32 devices in a mesh: dp: 8 (over z, y), row: 2 (over core), col: 2 (over x).
Axes of the slice: x: 2, y: 2, z: 4, core: 2. Of those that a mesh axis runs over, the one named last changes fastest.
Arguments:
- layer_input: bfloat16 [4096, 1024], P(('dp', 'row'), 'col'), as said below
- attn_gain: float32 [1024], P('col'), may hold values from 0.1 to 1.9
- mlp_gain: float32 [1024], P('col'), may hold values from 0.1 to 1.9
- qkv_weight: bfloat16 [1024, 3, 1024], P('col', None, 'row'), as said below
- proj_weight: bfloat16 [1024, 1024], P('row', 'col'), may hold values from -4 to 4
- inner_weight: bfloat16 [1024, 2, 2624], P('col', None, 'row'), may hold values from -0.1875 to 0.1875
- down_weight: bfloat16 [1024, 2624], P('col', 'row'), may hold values from -0.25 to 0.25
- cotangent: bfloat16 [4096, 1024], P(('dp', 'row'), 'col'), may hold values from -6 to 6
Outputs:
- layer_output: bfloat16 [4096, 1024], P(('dp', 'row'), 'col')
- input_grad: float32 [4096, 1024], P(('dp', 'row'), 'col')
- attn_gain_grad: float32 [1024], P('col')
- mlp_gain_grad: float32 [1024], P('col')
- qkv_grad: float32 [1024, 3, 1024], P(('col', 'dp'), None, 'row')
- proj_grad: float32 [1024, 1024], P(('row', 'dp'), 'col')
- inner_grad: float32 [1024, 2, 2624], P(('col', 'dp'), None, 'row')
- down_grad: float32 [1024, 2624], P(('col', 'dp'), 'row')
The draws below stay inside these ranges and needn't reach their ends.
Inputs may be any that keep to these rules, and one draw needn't show every extreme that they name: `layer_input`: real values. `qkv_weight`: real values.
All inputs are finite; a program needn't handle non-finite values.
Results may differ from the reference program's by a relative error of at most 0.01225.
Values may be sent and summed in bfloat16 or wider, within the bound.
A program may use at most 128 MiB of HBM per device.

```python
import jax
import jax.numpy as jnp
from jax import lax

D = 1024
HEADS = 16
FF = 2624
HD = 64
SEQ = 512
TOKENS = 4096


def draw_layer_input(key, part):
    subkeys = jax.random.split(key, 2)
    normal_draw = jax.random.normal(subkeys[0], (TOKENS, D), jnp.float32)
    rising = 3.0 ** (jnp.arange(D, dtype=jnp.float32) / D)
    columns = rising * jnp.exp(jax.random.uniform(subkeys[1], (D,), jnp.float32, -0.7, 0.7))
    return (normal_draw * columns[None, :]).astype(jnp.bfloat16)


def draw_qkv_weight(key, part):
    subkeys = jax.random.split(key, 1)
    normal_draw = jax.random.normal(subkeys[0], (D, 3, D), jnp.float32) * D ** (-0.5)
    return normal_draw.astype(jnp.bfloat16)


def with_spikes(entries, own_key, source, target, shards_of, factor):
    owner, partner = [(jnp.arange(entries.shape[dim]) // (entries.shape[dim] // shards_of)).reshape([-1 if axis == dim else 1 for axis in range(entries.ndim)]) for dim in (source, target)]
    chosen = jax.random.permutation(own_key, shards_of)[partner]
    strong = (owner == chosen) | (owner == (partner + shards_of // 2) % shards_of)
    return jnp.where(strong, factor * entries, entries)


def block_scale(rng, dims, cuts, low, top_value):
    level, own = 1.0, jax.random.fold_in(rng, 6)
    for axis_at, shards_of in cuts:
        steps = jnp.exp(jax.random.uniform(jax.random.fold_in(own, axis_at), (shards_of,), jnp.float32, low / len(cuts), top_value / len(cuts)))
        level = level * jnp.repeat(steps, dims[axis_at] // shards_of).reshape([-1 if axis == axis_at else 1 for axis in range(len(dims))])
    return level


def noise(rng, shape, spread, most, cuts=(), kind=jnp.bfloat16):
    level = block_scale(rng, shape, cuts, -0.22, 0.18) if cuts else 1.0
    drawn = jax.random.normal(rng, shape, jnp.float32) * spread * level
    return jnp.minimum(jnp.maximum(drawn, -most), most).astype(kind)


def gaussian_with(key, dims, deviation, limit, cuts, heavy, kind=jnp.bfloat16):
    values = deviation * jax.random.normal(key, dims, jnp.float32)
    if cuts:
        values = values * block_scale(key, dims, cuts, -0.22, 0.18)
    return jnp.clip(with_spikes(values, jax.random.fold_in(key, 3), *heavy), -limit, limit).astype(kind)


def setup_inputs(seed: int = 0) -> dict:
    key_list = jax.random.split(jax.random.key(seed), 9)
    return {
        "layer_input": draw_layer_input(jax.random.fold_in(key_list[8], 71), 0),
        "attn_gain": jnp.clip(1.0 + 0.18 * jax.random.normal(key_list[1], (D,), jnp.float32), 0.1, 1.9),
        "mlp_gain": jnp.clip(1.0 + 0.18 * jax.random.normal(key_list[2], (D,), jnp.float32), 0.1, 1.9),
        "qkv_weight": draw_qkv_weight(jax.random.fold_in(key_list[8], 71), 0),
        "proj_weight": noise(key_list[4], (D, D), (max(D // SEQ, 1)) ** -0.5, 4.0, ((0, 2), (1, 2))),
        "inner_weight": noise(key_list[5], (D, 2, FF), D ** -0.5, 0.1875, ((0, 2), (2, 2))),
        "down_weight": noise(key_list[6], (D, FF), (FF // 4) ** -0.5, 0.25, ((0, 2), (1, 2))),
        "cotangent": gaussian_with(key_list[7], (TOKENS, D), 1.0, 6.0, ((0, 16), (1, 2)), (0, 1, 16, 2.0)),
    }


ln_eps = 1e-05
rope_base = 160000.0
root_half = 0.7071067811865476
gauss_norm = 0.3989422804014327

def rope_tables(length, head_dim):
    half_dim = head_dim // 2
    rates = rope_base ** (-2.0 * jnp.arange(half_dim, dtype=jnp.float32) / head_dim)
    angles = jnp.arange(length, dtype=jnp.float32)[:, None] * rates[None, :]
    return (jnp.cos(angles), jnp.sin(angles))

def rotate(inputs, cos_table, sin_table):
    half_dim = inputs.shape[-1] // 2
    front_half = inputs[..., :half_dim]
    back_half = inputs[..., half_dim:]
    cosines = cos_table[:, None, :]
    sines = sin_table[:, None, :]
    return jnp.concatenate([front_half * cosines - back_half * sines, back_half * cosines + front_half * sines], axis=-1)

def unrotate(grads, cos_table, sin_table):
    half_dim = grads.shape[-1] // 2
    front_half = grads[..., :half_dim]
    back_half = grads[..., half_dim:]
    cosines = cos_table[:, None, :]
    sines = sin_table[:, None, :]
    return jnp.concatenate([front_half * cosines + back_half * sines, back_half * cosines - front_half * sines], axis=-1)

def attend(queries, key_rows, value_rows):
    score_scale = queries.shape[-1] ** (-0.5)
    scores = jnp.einsum('qhe,khe->hqk', queries.astype(jnp.float32), key_rows.astype(jnp.float32)) * score_scale
    highest = lax.optimization_barrier(jnp.max(scores, axis=-1, keepdims=True))
    log_total = highest + jnp.log(lax.optimization_barrier(jnp.sum(jnp.exp(scores - highest), axis=-1, keepdims=True)))
    probs_low = jnp.exp(scores - log_total).astype(jnp.bfloat16)
    attended = jnp.einsum('hqk,khe->qhe', probs_low.astype(jnp.float32), value_rows.astype(jnp.float32))
    return (attended.astype(jnp.bfloat16), log_total)

def attend_back(queries, key_rows, value_rows, attended, log_total, grad_attended):
    score_scale = queries.shape[-1] ** (-0.5)
    scores = jnp.einsum('qhe,khe->hqk', queries.astype(jnp.float32), key_rows.astype(jnp.float32)) * score_scale
    probs = jnp.exp(scores - log_total)
    probs_low = probs.astype(jnp.bfloat16)
    grad_wide = grad_attended.astype(jnp.float32)
    grad_values = jnp.einsum('hqk,qhe->khe', probs_low.astype(jnp.float32), grad_wide)
    grad_probs = jnp.einsum('qhe,khe->hqk', grad_wide, value_rows.astype(jnp.float32))
    row_dots = lax.optimization_barrier(jnp.sum(grad_wide * attended.astype(jnp.float32), axis=-1))
    grad_scores = (probs * (grad_probs - jnp.transpose(row_dots)[:, :, None]) * score_scale).astype(jnp.bfloat16)
    grad_queries = jnp.einsum('hqk,khe->qhe', grad_scores.astype(jnp.float32), key_rows.astype(jnp.float32))
    grad_keys = jnp.einsum('hqk,qhe->khe', grad_scores.astype(jnp.float32), queries.astype(jnp.float32))
    return (grad_queries, grad_keys, grad_values)

def norm_rows(stream):
    mean_rows = lax.optimization_barrier(jnp.mean(stream, axis=-1, keepdims=True))
    square_rows = lax.optimization_barrier(jnp.mean(stream * stream, axis=-1, keepdims=True))
    inverse = lax.rsqrt(square_rows - mean_rows * mean_rows + ln_eps)
    return ((stream - mean_rows) * inverse, inverse)

def norm_back(grad_normed, centred, inverse, gain, carried):
    grad_centred = grad_normed * gain
    mean_grad = lax.optimization_barrier(jnp.mean(grad_centred, axis=-1, keepdims=True))
    mean_proj = lax.optimization_barrier(jnp.mean(grad_centred * centred, axis=-1, keepdims=True))
    grad_stream = carried + inverse * (grad_centred - mean_grad - centred * mean_proj)
    return (grad_stream, lax.optimization_barrier(jnp.sum(grad_normed * centred, axis=0)))

def gelu_parts(gate_part):
    normal_cdf = 0.5 * (1.0 + lax.erf(gate_part * root_half))
    normal_pdf = gauss_norm * jnp.exp(-0.5 * gate_part * gate_part)
    return (normal_cdf, normal_pdf)

def reference(layer_input, attn_gain, mlp_gain, qkv_weight, proj_weight, inner_weight, down_weight, cotangent):
    cos_table, sin_table = rope_tables(SEQ, HD)
    qkv_flat = qkv_weight.reshape(D, 3 * D)
    inner_flat = inner_weight.reshape(D, 2 * FF)
    contract_rows = (((0,), (0,)), ((), ()))
    contract_cols = (((1,), (1,)), ((), ()))

    def one_sequence(totals, inputs):
        rows_in, grad_in = inputs
        stream = rows_in.astype(jnp.float32)
        centred_one, inverse_one = norm_rows(stream)
        normed_one = (centred_one * attn_gain).astype(jnp.bfloat16)
        projected = jnp.dot(normed_one, qkv_flat, preferred_element_type=jnp.float32).reshape(SEQ, 3, HEADS, HD)
        queries = rotate(projected[:, 0], cos_table, sin_table).astype(jnp.bfloat16)
        key_rows = rotate(projected[:, 1], cos_table, sin_table).astype(jnp.bfloat16)
        value_rows = projected[:, 2].astype(jnp.bfloat16)
        attended, log_total = attend(queries, key_rows, value_rows)
        attended_flat = attended.reshape(SEQ, D)
        middle = stream + jnp.dot(attended_flat, proj_weight, preferred_element_type=jnp.float32)
        centred_two, inverse_two = norm_rows(middle)
        normed_two = (centred_two * mlp_gain).astype(jnp.bfloat16)
        gate_up = jnp.dot(normed_two, inner_flat, preferred_element_type=jnp.float32).reshape(SEQ, 2, FF)
        gate_part = gate_up[:, 0]
        up_part = gate_up[:, 1]
        normal_cdf, normal_pdf = gelu_parts(gate_part)
        hidden = (gate_part * normal_cdf * up_part).astype(jnp.bfloat16)
        mlp_part = lax.dot_general(hidden, down_weight, contract_cols, preferred_element_type=jnp.float32)
        result = (middle + mlp_part).astype(jnp.bfloat16)
        grad_out = grad_in.astype(jnp.float32)
        down_term = lax.dot_general(grad_in, hidden, contract_rows, preferred_element_type=jnp.float32)
        grad_hidden = jnp.dot(grad_in, down_weight, preferred_element_type=jnp.float32)
        grad_gate_up = jnp.stack([grad_hidden * up_part * (normal_cdf + gate_part * normal_pdf), grad_hidden * gate_part * normal_cdf], axis=1).astype(jnp.bfloat16)
        grad_flat = grad_gate_up.reshape(SEQ, 2 * FF)
        inner_term = lax.dot_general(normed_two, grad_flat, contract_rows, preferred_element_type=jnp.float32).reshape(D, 2, FF)
        grad_normed_two = lax.dot_general(grad_flat, inner_flat, contract_cols, preferred_element_type=jnp.float32)
        grad_middle, gain_two = norm_back(grad_normed_two, centred_two, inverse_two, mlp_gain, grad_out)
        grad_low = grad_middle.astype(jnp.bfloat16)
        proj_term = lax.dot_general(attended_flat, grad_low, contract_rows, preferred_element_type=jnp.float32)
        grad_attended = lax.dot_general(grad_low, proj_weight, contract_cols, preferred_element_type=jnp.float32)
        grad_attended = grad_attended.astype(jnp.bfloat16).reshape(SEQ, HEADS, HD)
        grad_queries, grad_keys, grad_values = attend_back(queries, key_rows, value_rows, attended, log_total, grad_attended)
        grad_qkv = jnp.stack([unrotate(grad_queries, cos_table, sin_table), unrotate(grad_keys, cos_table, sin_table), grad_values], axis=1)
        grad_qkv = grad_qkv.astype(jnp.bfloat16).reshape(SEQ, 3 * D)
        qkv_term = lax.dot_general(normed_one, grad_qkv, contract_rows, preferred_element_type=jnp.float32).reshape(D, 3, D)
        grad_normed_one = lax.dot_general(grad_qkv, qkv_flat, contract_cols, preferred_element_type=jnp.float32)
        grad_stream, gain_one = norm_back(grad_normed_one, centred_one, inverse_one, attn_gain, grad_middle)
        totals = (totals[0] + gain_one, totals[1] + gain_two, totals[2] + qkv_term, totals[3] + proj_term, totals[4] + inner_term, totals[5] + down_term)
        return (totals, (result, grad_stream))
    seq_count = TOKENS // SEQ
    start_totals = (jnp.zeros((D,), jnp.float32), jnp.zeros((D,), jnp.float32), jnp.zeros((D, 3, D), jnp.float32), jnp.zeros((D, D), jnp.float32), jnp.zeros((D, 2, FF), jnp.float32), jnp.zeros((D, FF), jnp.float32))
    totals, outputs = lax.scan(one_sequence, start_totals, (layer_input.reshape(seq_count, SEQ, D), cotangent.reshape(seq_count, SEQ, D)))
    return (outputs[0].reshape(TOKENS, D), outputs[1].reshape(TOKENS, D), totals[0], totals[1], totals[2], totals[3], totals[4], totals[5])
```

```python
import jax
import jax.numpy as jnp
from jax import lax
from jax.sharding import PartitionSpec as P

HD = 64
SEQ = 512

ln_eps = 1e-05
rope_base = 160000.0
root_half = 0.7071067811865476
gauss_norm = 0.3989422804014327
bf16 = jnp.bfloat16
f32 = jnp.float32


def rope_tables(length, head_dim):
    half_dim = head_dim // 2
    rates = rope_base ** (-2.0 * jnp.arange(half_dim, dtype=f32) / head_dim)
    angles = jnp.arange(length, dtype=f32)[:, None] * rates[None, :]
    return (jnp.cos(angles), jnp.sin(angles))


def rotate(inputs, cos_table, sin_table):
    half_dim = inputs.shape[-1] // 2
    front, back = inputs[..., :half_dim], inputs[..., half_dim:]
    cosines, sines = cos_table[:, None, :], sin_table[:, None, :]
    return jnp.concatenate(
        [front * cosines - back * sines, back * cosines + front * sines], axis=-1
    )


def attend(queries, key_rows, value_rows):
    scale = queries.shape[-1] ** (-0.5)
    scores = jnp.einsum("sqhe,skhe->shqk", queries, key_rows, preferred_element_type=f32) * scale
    highest = jnp.max(scores, axis=-1, keepdims=True)
    log_total = highest + jnp.log(jnp.sum(jnp.exp(scores - highest), axis=-1, keepdims=True))
    probs_low = jnp.exp(scores - log_total).astype(bf16)
    attended = jnp.einsum("shqk,skhe->sqhe", probs_low, value_rows, preferred_element_type=f32)
    return attended.astype(bf16), log_total


def attend_back(queries, key_rows, value_rows, attended, log_total, grad_attended):
    scale = queries.shape[-1] ** (-0.5)
    scores = jnp.einsum("sqhe,skhe->shqk", queries, key_rows, preferred_element_type=f32) * scale
    probs = jnp.exp(scores - log_total)
    probs_low = probs.astype(bf16)
    grad_values = jnp.einsum(
        "shqk,sqhe->skhe", probs_low, grad_attended, preferred_element_type=f32
    )
    grad_probs = jnp.einsum(
        "sqhe,skhe->shqk", grad_attended, value_rows, preferred_element_type=f32
    )
    row_dots = jnp.sum(grad_attended.astype(f32) * attended.astype(f32), axis=-1)
    row_dots = jnp.transpose(row_dots, (0, 2, 1))[..., None]
    grad_scores = (probs * (grad_probs - row_dots) * scale).astype(bf16)
    grad_queries = jnp.einsum("shqk,skhe->sqhe", grad_scores, key_rows, preferred_element_type=f32)
    grad_keys = jnp.einsum("shqk,sqhe->skhe", grad_scores, queries, preferred_element_type=f32)
    return grad_queries, grad_keys, grad_values


def gelu_parts(gate_part):
    normal_cdf = 0.5 * (1.0 + lax.erf(gate_part * root_half))
    normal_pdf = gauss_norm * jnp.exp(-0.5 * gate_part * gate_part)
    return normal_cdf, normal_pdf


def dot_nn(a, b):
    return jnp.dot(a, b, preferred_element_type=f32)


def dot_tn(a, b):
    return lax.dot_general(a, b, (((0,), (0,)), ((), ())), preferred_element_type=f32)


def dot_nt(a, b):
    return lax.dot_general(a, b, (((1,), (1,)), ((), ())), preferred_element_type=f32)


def col_swap(block):
    return lax.ppermute(block, "col", [(0, 1), (1, 0)])


def row_swap(block):
    return lax.ppermute(block, "row", [(0, 1), (1, 0)])


def halves_own(block, at, axis):
    half = block.shape[axis] // 2
    low = lax.slice_in_dim(block, 0, half, axis=axis)
    high = lax.slice_in_dim(block, half, 2 * half, axis=axis)
    first = at == 0
    return jnp.where(first, low, high), jnp.where(first, high, low)


def whole_order(own, other, at, axis):
    first = at == 0
    return jnp.concatenate([jnp.where(first, own, other), jnp.where(first, other, own)], axis=axis)


def row_scatter(part):
    local_rows = part.shape[0] // 2
    return part[:local_rows] + row_swap(part[local_rows:].astype(bf16)).astype(f32)


def col_total(part):
    width = part.shape[1] // 2
    other = col_swap(part.astype(bf16)).astype(f32)
    return part + jnp.concatenate([other[:, width:], other[:, :width]], axis=1)


def dp_scatter(terms):
    count = lax.axis_size("dp")
    bits = count.bit_length() - 1
    if count != 1 << bits:
        return lax.psum_scatter(terms, "dp", scatter_dimension=1, tiled=False)
    at = lax.axis_index("dp")
    lead, rest = terms.shape[0], terms.shape[2:]
    terms = terms.reshape((lead,) + (2,) * bits + rest)
    for bit in range(bits):
        axis = bits - bit
        mine = (at >> bit) & 1
        keep = lax.dynamic_index_in_dim(terms, mine, axis, keepdims=False)
        send = lax.dynamic_index_in_dim(terms, 1 - mine, axis, keepdims=False)
        pairs = [(i, i ^ (1 << bit)) for i in range(count)]
        terms = keep + lax.ppermute(send.astype(bf16), "dp", pairs).astype(f32)
    return terms


def width_grad(term, at):
    count = lax.axis_size("dp")
    rows = term.shape[0] // (2 * count)
    parts = dp_scatter(term.reshape(2, count, rows, term.shape[1]))
    other = col_swap(parts[1].astype(bf16)).astype(f32)
    return parts[0], other


def norm_rows(stream):
    width = stream.shape[1]
    mean_rows = jnp.sum(stream, axis=1, keepdims=True) / width
    square_rows = jnp.sum(stream * stream, axis=1, keepdims=True) / width
    inverse = lax.rsqrt(square_rows - mean_rows * mean_rows + ln_eps)
    return (stream - mean_rows) * inverse, inverse


def norm_back(grad_normed, centred, inverse, gain, carried):
    width = centred.shape[1]
    grad_centred = grad_normed * gain
    mean_grad = jnp.sum(grad_centred, axis=1, keepdims=True) / width
    mean_proj = jnp.sum(grad_centred * centred, axis=1, keepdims=True) / width
    grad_stream = carried + inverse * (grad_centred - mean_grad - centred * mean_proj)
    return grad_stream, jnp.sum(grad_normed * centred, axis=0)


def local(
    layer_input, attn_gain, mlp_gain, qkv_weight, proj_weight, inner_weight, down_weight, cotangent
):
    assert lax.axis_size("row") == 2 and lax.axis_size("col") == 2
    at = lax.axis_index("col")
    row_at = lax.axis_index("row")
    local_rows, width = layer_input.shape
    group_rows = 2 * local_rows
    seq_count = group_rows // SEQ
    assert seq_count == 1 or local_rows % SEQ == 0
    units = qkv_weight.shape[2] // 2
    heads = units // HD

    def widen(block):
        return jnp.concatenate([block, col_swap(block)], axis=1)

    def all_tokens(block):
        return jnp.concatenate([block, row_swap(block)], axis=0)

    stream = widen(layer_input).astype(f32)
    gains = jnp.stack([attn_gain, mlp_gain])
    gains = widen(gains)
    gain_a, gain_m = gains[0:1], gains[1:2]

    def fetch(block, unit_axis, width_axis):
        mine, theirs = halves_own(block, at, unit_axis)
        return jnp.concatenate([mine, col_swap(theirs)], axis=width_axis)

    qkv_flat = jnp.concatenate(
        [
            jnp.concatenate(pair, axis=1)
            for pair in [
                [halves_own(qkv_weight[:, j], at, 1)[side] for j in range(3)] for side in (0, 1)
            ]
        ],
        axis=0,
    )
    qkv_full = jnp.concatenate([qkv_flat[:width], col_swap(qkv_flat[width:])], axis=0)
    grad_rows = widen(cotangent)
    proj_full = fetch(proj_weight, 0, 1)
    gate_full = fetch(inner_weight[:, 0], 1, 0)
    up_full = fetch(inner_weight[:, 1], 1, 0)
    down_full = fetch(down_weight, 1, 0)

    cos_table, sin_table = rope_tables(SEQ, HD)
    if seq_count == 1:
        turn = lambda table: jnp.where(row_at == 0, table, jnp.roll(table, -local_rows, axis=0))
        cos_table, sin_table = turn(cos_table), turn(sin_table)

    centred_one, inverse_one = norm_rows(stream)
    full_one = all_tokens((centred_one * gain_a).astype(bf16))
    projected = dot_nn(full_one, qkv_full)
    split = lambda block: block.reshape(seq_count, SEQ, heads, HD)
    queries = rotate(split(projected[:, :units]), cos_table, sin_table).astype(bf16)
    key_rows = rotate(split(projected[:, units : 2 * units]), cos_table, sin_table).astype(bf16)
    value_rows = split(projected[:, 2 * units :]).astype(bf16)
    attended, log_total = attend(queries, key_rows, value_rows)
    attended_flat = attended.reshape(group_rows, units)
    middle = stream + col_total(row_scatter(dot_nn(attended_flat, proj_full)))

    centred_two, inverse_two = norm_rows(middle)
    full_two = all_tokens((centred_two * gain_m).astype(bf16))
    gate_part = dot_nn(full_two, gate_full)
    up_part = dot_nn(full_two, up_full)
    normal_cdf, normal_pdf = gelu_parts(gate_part)
    hidden = (gate_part * normal_cdf * up_part).astype(bf16)

    grad_full = all_tokens(grad_rows)
    grad_hidden = dot_nn(grad_full, down_full)
    grad_gate = (grad_hidden * up_part * (normal_cdf + gate_part * normal_pdf)).astype(bf16)
    grad_up = (grad_hidden * gate_part * normal_cdf).astype(bf16)
    grad_normed_two = col_total(
        row_scatter(dot_nt(grad_gate, gate_full) + dot_nt(grad_up, up_full))
    )

    mlp_part = row_scatter(dot_nt(hidden, down_full))
    mlp_total = mlp_part[:, :width] + col_swap(mlp_part[:, width:].astype(bf16)).astype(f32)
    result = (middle[:, :width] + mlp_total).astype(bf16)
    down_grad = jnp.concatenate([*whole_pair(width_grad(dot_tn(grad_full, hidden), at), at)], axis=1)
    gate_grad = jnp.concatenate(
        [*whole_pair(width_grad(dot_tn(full_two, grad_gate), at), at)], axis=1
    )
    up_grad = jnp.concatenate([*whole_pair(width_grad(dot_tn(full_two, grad_up), at), at)], axis=1)
    inner_grad = jnp.stack([gate_grad, up_grad], axis=1)

    grad_middle, gain_two = norm_back(
        grad_normed_two, centred_two, inverse_two, gain_m, grad_rows.astype(f32)
    )
    grad_low_full = all_tokens(grad_middle.astype(bf16))
    grad_attended = split(dot_nt(grad_low_full, proj_full).astype(bf16))
    proj_term = dot_tn(attended_flat, grad_low_full)
    proj_other = col_swap(proj_term[:, width:].astype(bf16)).astype(f32)
    proj_rows = whole_order(proj_term[:, :width], proj_other, at, 0)
    count = lax.axis_size("dp")
    proj_grad = dp_scatter(proj_rows.reshape(1, count, proj_rows.shape[0] // count, width))[0]

    grad_queries, grad_keys, grad_values = attend_back(
        queries, key_rows, value_rows, attended, log_total, grad_attended
    )
    flat = lambda block: block.astype(bf16).reshape(group_rows, units)
    grad_qkv = jnp.concatenate(
        [
            flat(rotate(grad_queries, cos_table, -sin_table)),
            flat(rotate(grad_keys, cos_table, -sin_table)),
            flat(grad_values),
        ],
        axis=1,
    )
    grad_normed_one = col_total(row_scatter(dot_nt(grad_qkv, qkv_full)))
    qkv_low, qkv_high = whole_pair(width_grad(dot_tn(full_one, grad_qkv), at), at)
    qkv_grad = jnp.stack(
        [
            jnp.concatenate(
                [block[:, j * units : (j + 1) * units] for block in (qkv_low, qkv_high)], axis=1
            )
            for j in range(3)
        ],
        axis=1,
    )
    grad_stream, gain_one = norm_back(
        grad_normed_one, centred_one, inverse_one, gain_a, grad_middle
    )
    gain_totals = lax.psum(jnp.stack([gain_one[:width], gain_two[:width]]), ("dp", "row"))
    return (
        result,
        grad_stream[:, :width],
        gain_totals[0],
        gain_totals[1],
        qkv_grad,
        proj_grad,
        inner_grad,
        down_grad,
    )


def whole_pair(pair, at):
    own, other = pair
    first = at == 0
    return jnp.where(first, own, other), jnp.where(first, other, own)


def solution(mesh):
    in_specs = (
        P(("dp", "row"), "col"),
        P("col"),
        P("col"),
        P("col", None, "row"),
        P("row", "col"),
        P("col", None, "row"),
        P("col", "row"),
        P(("dp", "row"), "col"),
    )
    out_specs = (
        P(("dp", "row"), "col"),
        P(("dp", "row"), "col"),
        P("col"),
        P("col"),
        P(("col", "dp"), None, "row"),
        P(("row", "dp"), "col"),
        P(("col", "dp"), None, "row"),
        P(("col", "dp"), "row"),
    )
    return jax.shard_map(local, mesh=mesh, in_specs=in_specs, out_specs=out_specs, check_vma=False)
```
